32 devices in a mesh: lat: 4 (over y, x), ord: 8 (over z, core).
Axes of the slice: x: 2, y: 2, z: 4, core: 2. Of those that a mesh axis runs over, the one named last changes fastest.
Arguments:
- heights: bfloat16 [512, 43200], P(('lat', 'ord')), may hold values from -1.5 to 1.5
- panels: bfloat16 [512, 5120, 128], P('lat', 'ord'), may hold values from -0.25 to 0.25
- ord_slot: int32 [5120], replicated, may hold values from 0 to 5119, each once
- cutoffs: int32 [5120], P('ord'), may hold values from 13360 to 21599
Outputs:
- gravity: float32 [512, 43200], P(('lat', 'ord'))
The draws below stay inside these ranges and needn't reach their ends.
Inputs may be any that keep to these rules, and one draw needn't show every extreme that they name: `ord_slot`: a permutation of the order slots.
All inputs are finite; a program needn't handle non-finite values.
Results may differ from the reference program's by a relative error of at most 0.0039.
Values may be sent and summed in bfloat16 or wider, within the bound.
No kernel may reach another device: no remote copies, remote signals or barrier semaphores. Data moves between devices by JAX's collectives and lax.ppermute only.
A program may use at most 192 MiB of HBM per device.

```python
import math
import jax
import jax.numpy as jnp
from jax import lax

ORDERS = 5120
DEG = 128
NMAX = 21600
LON = 43200
CYCLES = 512


def with_ends(result, stream_key, low, largest):
    dims = result.shape
    place = [jax.random.randint(jax.random.fold_in(stream_key, axis), (), 0, dims[axis]) for axis in range(len(dims))]
    result = result.at[tuple(place)].set(low)
    longest = dims.index(max(dims))
    place[longest] = (place[longest] + 1) % dims[longest]
    return result.at[tuple(place)].set(largest)


def block_levels(key, shape, shards, low, top_value):
    def one(position, blocks):
        draws = jax.random.uniform(jax.random.fold_in(jax.random.fold_in(key, 6), position), (blocks,), jnp.float32, low / len(shards), top_value / len(shards))
        return jnp.repeat(jnp.exp(draws), shape[position] // blocks).reshape((-1,) + (1,) * (len(shape) - position - 1))

    loudness = one(*shards[0])
    for cut in shards[1:]:
        loudness = loudness * one(*cut)
    return loudness


def bell_draw(rng, dims, spread, most, shards=(), held_as=jnp.bfloat16):
    drawn = spread * jax.random.normal(rng, dims, jnp.float32)
    if shards:
        drawn = drawn * block_levels(rng, dims, shards, -0.22, 0.18)
    return jnp.clip(drawn, -most, most).astype(held_as)


def setup_inputs(seed: int = 0) -> dict:
    streams_of = jax.random.split(jax.random.key(seed), 5)
    return {
        "heights": jnp.clip(jax.random.uniform(streams_of[0], (CYCLES, LON), jnp.float32, -1.5, 1.5) * block_levels(streams_of[0], (CYCLES, LON), ((0, 32),), -0.4, 0.0), -1.5, 1.5).astype(jnp.bfloat16),
        "panels": bell_draw(streams_of[1], (CYCLES, ORDERS, DEG), CYCLES ** -0.5, 0.25, ((0, 4), (1, 8))),
        "ord_slot": jax.random.permutation(streams_of[2], ORDERS).astype(jnp.int32),
        "cutoffs": with_ends(jax.random.randint(streams_of[3], (ORDERS,), (NMAX + ORDERS) // 2, NMAX), jax.random.fold_in(streams_of[3], 1), (NMAX + ORDERS) // 2, NMAX - 1).astype(jnp.int32),
    }


def reference(heights, panels, ord_slot, cutoffs):
    level = heights.astype(jnp.float32)
    cycles = level.shape[0]
    scale_in = 1.0 / math.sqrt(LON)
    pieces = []
    value = level
    for power in range(3):
        if power > 0:
            value = value * level
        spectrum = jnp.fft.rfft(value, axis=1)[:, 1:ORDERS + 1] * scale_in
        pieces.append(jnp.real(spectrum)[:, ord_slot])
        pieces.append(jnp.imag(spectrum)[:, ord_slot])
    picked = jnp.stack(pieces).astype(jnp.bfloat16)
    picked = lax.optimization_barrier(picked)
    stride = (NMAX - ORDERS) // DEG
    degree_int = (ORDERS + jnp.arange(DEG, dtype=jnp.int32) * stride).astype(jnp.int32)
    degree = degree_int.astype(jnp.float32)
    factors = jnp.stack([jnp.ones_like(degree), (degree + 2.0) / (2.0 * NMAX), (degree + 2.0) * (degree + 1.0) / (6.0 * NMAX * NMAX)])
    block = math.gcd(ORDERS, 256)

    def one_block(index):
        start = (index * block).astype(jnp.int32)
        panel = lax.dynamic_slice_in_dim(panels, start, block, 1).astype(jnp.float32)
        spectra = lax.dynamic_slice_in_dim(picked, start, block, 2).astype(jnp.float32)
        limits = lax.dynamic_slice_in_dim(cutoffs, start, block, 0)
        sums = jnp.einsum('xrk,rkn->xkn', spectra, panel)
        folded = lax.optimization_barrier(jnp.sum(sums.reshape(3, 2, block, DEG) * factors[:, None, None, :], axis=0))
        keep = (degree_int[None, :] <= limits[:, None]).astype(jnp.float32)
        coeffs = (folded * keep).astype(jnp.bfloat16)
        coeffs = lax.optimization_barrier(coeffs).astype(jnp.float32)
        return jnp.einsum('rkn,ckn->crk', panel, coeffs)
    outputs = lax.map(one_block, jnp.arange(ORDERS // block, dtype=jnp.int32))
    synthesis = outputs.transpose(1, 2, 0, 3).reshape(2, cycles, ORDERS)
    half = LON // 2 + 1
    target = (ord_slot + 1).astype(jnp.int32)
    full_real = jnp.zeros((cycles, half), synthesis.dtype).at[:, target].set(synthesis[0])
    full_imag = jnp.zeros((cycles, half), synthesis.dtype).at[:, target].set(synthesis[1])
    field = jnp.fft.irfft(full_real + 1j * full_imag, n=LON, axis=1) * (LON / 2.0)
    return field * math.sqrt(CYCLES / (DEG * ORDERS))
```

```python
import functools
import math

import jax
import jax.numpy as jnp
import ml_dtypes
import numpy as np
from jax import lax
from jax.experimental import pallas as pl
from jax.experimental.pallas import tpu as pltpu
from jax.sharding import PartitionSpec as P

SLOW = 180
FAST = 240
HALF = SLOW // 2 + 1
KPAD = 96
QPAD = 32
APAD = 184
FPITCH = 136
IPITCH = 200
BATCH = 5
LANES = 256
ORDERS = 5120
DEG = 128
NMAX = 21600
LON = SLOW * FAST
f32 = jnp.float32
bf16 = jnp.bfloat16


def halves(table):
    high = table.astype(ml_dtypes.bfloat16)
    return high, (table - high.astype(np.float64)).astype(ml_dtypes.bfloat16)


def split(x):
    high = x.astype(bf16)
    return high, (x - high.astype(f32)).astype(bf16)


def angles(total, phase):
    return 2.0 * np.pi / total * (phase % total).astype(np.float64)


@functools.lru_cache
def forward_tables():
    k = np.arange(HALF)[:, None]
    a = np.arange(SLOW)[None, :]
    first = np.zeros((2 * KPAD, SLOW))
    first[:HALF] = np.cos(angles(SLOW, k * a))
    first[KPAD : KPAD + HALF] = -np.sin(angles(SLOW, k * a))
    j = np.arange(FAST)[None, :]
    twist = np.zeros((2, KPAD, FAST), np.float32)
    twist[0, :HALF] = np.cos(angles(LON, k * j)) / math.sqrt(LON)
    twist[1, :HALF] = np.sin(angles(LON, k * j)) / math.sqrt(LON)
    q = np.arange(QPAD)[:, None]
    last = np.concatenate([np.cos(angles(FAST, q * j)), np.sin(angles(FAST, q * j))])
    return np.concatenate(halves(first)), twist, np.concatenate(halves(last))


@functools.lru_cache
def inverse_tables(scale):
    q = np.arange(QPAD)[:, None]
    j = np.arange(FAST)[None, :]
    first = np.zeros((QPAD, 2 * LANES))
    first[:, :FAST] = np.cos(angles(FAST, q * j))
    first[:, LANES : LANES + FAST] = np.sin(angles(FAST, q * j))
    k = np.arange(HALF)[:, None]
    twist = np.zeros((2, KPAD, LANES), np.float32)
    twist[0, :HALF, :FAST] = scale * np.cos(angles(LON, k * j))
    twist[1, :HALF, :FAST] = scale * np.sin(angles(LON, k * j))
    a = np.arange(SLOW)[:, None]
    last = np.zeros((APAD, 2 * KPAD))
    last[:SLOW, :HALF] = np.cos(angles(SLOW, a * k.T))
    last[:SLOW, KPAD : KPAD + HALF] = -np.sin(angles(SLOW, a * k.T))
    high, low = halves(first)
    return np.concatenate([high, high, low]), twist, np.concatenate(halves(last))


def swap_blocks(x):
    shape = (x.shape[0] // 8, 8, 128)
    x = x.reshape(shape)
    rows = lax.broadcasted_iota(jnp.int32, shape, 1)
    cols = lax.broadcasted_iota(jnp.int32, shape, 2) // 16
    for bit in (4, 2, 1):
        moved = pltpu.roll(pltpu.roll(x, 8 - bit, 1), 16 * bit, 2)
        if bit < 4:
            down = pltpu.roll(pltpu.roll(x, bit, 1), 128 - 16 * bit, 2)
            moved = jnp.where((rows & bit) == 0, moved, down)
        x = jnp.where((rows & bit) == (cols & bit), x, moved)
    return x.reshape(shape[0] * 8, 128)


def forward_kernel(
    per_chunk, chunks, addr_ref, x_ref, first_ref, twist_ref, last_ref, out_ref, ya, yb, z, g
):
    cycles = x_ref.shape[0]
    rest = FAST - 128

    def first_stage(r, carry):
        level = x_ref[r].astype(f32)
        square = level * level
        for p, value in enumerate((level, square, square * level)):
            high, low = split(value)
            o = jnp.dot(first_ref[...], high, preferred_element_type=f32)
            o = o[: 2 * KPAD] + o[2 * KPAD :]
            if p > 0:
                o = o + jnp.dot(first_ref[: 2 * KPAD], low, preferred_element_type=f32)
            real, imag = o[:KPAD], o[KPAD:]
            cosine, sine = twist_ref[0], twist_ref[1]
            turned = (real * cosine + imag * sine, imag * cosine - real * sine)
            for c in range(2):
                row = c * 64 + p * cycles + r
                ya[pl.ds(row, KPAD, stride=FPITCH), :] = turned[c][:, :128]
                yb[pl.ds(row, KPAD, stride=FPITCH), 0:rest] = turned[c][:, 128:]
        return carry

    lax.fori_loop(0, cycles, first_stage, 0)
    flip = jnp.where(lax.broadcasted_iota(jnp.int32, (QPAD, 128), 1) < 64, 1.0, -1.0)

    def second_stage(k, carry):
        base = pl.multiple_of(k * FPITCH, 8)
        value = jnp.concatenate([ya[pl.ds(base, 128), :], yb[pl.ds(base, 128), 0:rest]], 1)
        high, low = split(value)
        dims = (((1,), (1,)), ((), ()))
        o = lax.dot_general(last_ref[...], high, dims, preferred_element_type=f32)
        o = o[: 2 * QPAD] + o[2 * QPAD :]
        o = o + lax.dot_general(last_ref[: 2 * QPAD], low, dims, preferred_element_type=f32)
        oc = o[:QPAD]
        os = pltpu.roll(o[QPAD:], 64, 1)
        place = pl.multiple_of(k * 64, 64)
        z[pl.ds(place, QPAD), :] = oc + flip * os
        z[pl.ds(place + QPAD, QPAD), :] = flip * oc - os
        return carry

    lax.fori_loop(0, HALF, second_stage, 0, unroll=7)

    def pick(b, carry):
        for i in range(128 * BATCH):
            g[pl.ds(i, 1), :] = z[pl.ds(addr_ref[b * 128 * BATCH + i], 1), :]
        for n in range(BATCH):
            turned = g[128 * n : 128 * n + 128, :].T
            wanted = jnp.concatenate([turned[:48], turned[64:112]], 0)
            turned = swap_blocks(wanted)
            for u in range(8 // per_chunk):
                columns = []
                for h in range(2):
                    parts = []
                    for x in range(6):
                        row = (x % 2) * 48 + (x // 2) * 16 + h * 8 + u * per_chunk
                        parts.append(turned[row : row + per_chunk])
                    columns.append(jnp.concatenate(parts, 0))
                piece = (b * BATCH + n) * (8 // per_chunk) + u
                out_ref[piece // chunks, piece % chunks] = jnp.concatenate(columns, 1).astype(bf16)
        return carry

    lax.fori_loop(0, ORDERS // 128 // BATCH, pick, 0)


def forward(heights, addr, dests, slots):
    cycles = heights.shape[0]
    chunk = math.gcd(slots, 128)
    chunks, per_chunk = slots // chunk, chunk // 16
    first, twist, last = forward_tables()
    vmem = pl.BlockSpec(memory_space=pltpu.VMEM)
    return pl.pallas_call(
        functools.partial(forward_kernel, per_chunk, chunks),
        in_specs=[pl.BlockSpec(memory_space=pltpu.SMEM)] + [vmem] * 4,
        out_specs=vmem,
        out_shape=jax.ShapeDtypeStruct((dests, chunks, 6 * per_chunk, 16 * cycles), bf16),
        scratch_shapes=[
            pltpu.VMEM((KPAD * FPITCH, 128), f32),
            pltpu.VMEM((KPAD * FPITCH, 128), f32),
            pltpu.VMEM((KPAD * 64, 128), f32),
            pltpu.VMEM((128 * BATCH, 128), f32),
        ],
        name="forward",
    )(addr, heights.reshape(cycles, SLOW, FAST), first, twist, last)


def analysis_kernel(per_chunk, p_ref, panels_ref, q_ref, out_ref):
    sources = p_ref.shape[0]
    wide = p_ref.shape[3]
    span = sources * wide
    shape = (16, wide)
    mask = lax.broadcasted_iota(jnp.int32, shape, 1) % 16 == lax.broadcasted_iota(
        jnp.int32, shape, 0
    )
    owners = out_ref.shape[0]
    size = out_ref.shape[3]
    terms = [[], []]
    for kb in range(per_chunk):
        w = panels_ref[:, kb * 16 : (kb + 1) * 16, :].reshape(span, DEG)
        rows = []
        for x in range(6):
            row = x * per_chunk + kb
            cols = []
            for s in range(sources):
                line = jnp.broadcast_to(p_ref[s, 0, row : row + 1, :], shape)
                cols.append(jnp.where(mask, line, jnp.zeros((), bf16)))
            rows.append(jnp.concatenate(cols, 1))
        s = jnp.dot(jnp.concatenate(rows, 0), w, preferred_element_type=f32)
        for c in range(2):
            terms[c].append(
                q_ref[0:1] * s[16 * c : 16 * c + 16]
                + q_ref[1:2] * s[32 + 16 * c : 48 + 16 * c]
                + q_ref[2:3] * s[64 + 16 * c : 80 + 16 * c]
            )
    for c in range(2):
        total = jnp.concatenate(terms[c], 0)
        for owner in range(owners):
            out_ref[owner, 0, c] = total[owner * size : (owner + 1) * size].astype(out_ref.dtype)


def analysis(picked, panels, factors, owners):
    sources, chunks, rows, wide = picked.shape
    per_chunk = rows // 6
    chunk = per_chunk * 16
    size = chunk // owners
    return pl.pallas_call(
        functools.partial(analysis_kernel, per_chunk),
        grid=(chunks,),
        in_specs=[
            pl.BlockSpec((sources, 1, rows, wide), lambda i: (0, i, 0, 0)),
            pl.BlockSpec((panels.shape[0], chunk, DEG), lambda i: (0, i, 0)),
            pl.BlockSpec((8, DEG), lambda i: (0, 0)),
        ],
        out_specs=pl.BlockSpec((owners, 1, 2, size, DEG), lambda i: (0, i, 0, 0, 0)),
        out_shape=jax.ShapeDtypeStruct((owners, chunks, 2, size, DEG), bf16),
        name="analysis",
    )(picked, panels, factors)


def synthesis_kernel(per_chunk, me_ref, *refs):
    coeff_refs, panels_ref, out_ref = refs[:-2], refs[-2], refs[-1]
    dests = out_ref.shape[0]
    wide = out_ref.shape[3]
    span = dests * wide
    owners = len(coeff_refs)
    mask = lax.broadcasted_iota(jnp.int32, (16, span), 1) % 16 == lax.broadcasted_iota(
        jnp.int32, (16, span), 0
    )
    me = me_ref[0]
    full = []
    for c in range(2):
        parts = []
        for owner in range(owners):
            away = lax.rem(me - owner + owners, owners)
            piece = coeff_refs[0][0, c]
            for s in range(1, owners):
                piece = jnp.where(away == s, coeff_refs[s][0, c], piece)
            parts.append(piece)
        full.append(jnp.concatenate(parts, 0))
    lines = [[], []]
    for kb in range(per_chunk):
        w = panels_ref[:, kb * 16 : (kb + 1) * 16, :].reshape(span, DEG)
        both = jnp.concatenate([full[c][kb * 16 : (kb + 1) * 16] for c in range(2)], 0)
        o = lax.dot_general(both, w, (((1,), (1,)), ((), ())), preferred_element_type=f32)
        for c in range(2):
            kept = jnp.where(mask, o[16 * c : 16 * c + 16], 0.0)
            lines[c].append(jnp.sum(kept, axis=0, keepdims=True))
    block = jnp.concatenate(lines[0] + lines[1], 0).astype(out_ref.dtype)
    for d in range(dests):
        out_ref[d, 0] = block[:, d * wide : (d + 1) * wide]


def synthesis(me, pieces, panels, dests, wide):
    chunks, _, size, _ = pieces[0].shape
    chunk = size * len(pieces)
    per_chunk = chunk // 16
    piece_spec = pl.BlockSpec((1, 2, size, DEG), lambda i: (i, 0, 0, 0))
    return pl.pallas_call(
        functools.partial(synthesis_kernel, per_chunk),
        grid=(chunks,),
        in_specs=[pl.BlockSpec(memory_space=pltpu.SMEM)]
        + [piece_spec] * len(pieces)
        + [pl.BlockSpec((panels.shape[0], chunk, DEG), lambda i: (0, i, 0))],
        out_specs=pl.BlockSpec((dests, 1, 2 * per_chunk, wide), lambda i: (0, i, 0, 0)),
        out_shape=jax.ShapeDtypeStruct((dests, chunks, 2 * per_chunk, wide), bf16),
        name="synthesis",
    )(me, *pieces, panels)


def inverse_kernel(
    per_chunk, chunks, addr_ref, s_ref, first_ref, twist_ref, last_ref, out_ref, table, g, va, vb
):
    cycles = out_ref.shape[0]
    table[...] = jnp.zeros(table.shape, f32)
    g[...] = jnp.zeros(g.shape, f32)

    def place(b, carry):
        for n in range(BATCH):
            rows = []
            for c in range(2):
                for h in range(2):
                    for u in range(8 // per_chunk):
                        piece = (b * BATCH + n) * (8 // per_chunk) + u
                        block = s_ref[piece // chunks, piece % chunks].astype(f32)
                        rows.append(
                            block[c * per_chunk : (c + 1) * per_chunk, h * 128 : (h + 1) * 128]
                        )
            turned = swap_blocks(jnp.concatenate(rows, 0))
            g[128 * n : 128 * n + 128, : 2 * cycles] = turned.T
        for i in range(128 * BATCH):
            table[pl.ds(addr_ref[b * 128 * BATCH + i], 1), :] = g[pl.ds(i, 1), :]
        return carry

    lax.fori_loop(0, ORDERS // 128 // BATCH, place, 0)

    def first_stage(pair, carry):
        total = None
        for e in range(2):
            base = pl.multiple_of((2 * pair + e) * 64, 64)
            plus = table[pl.ds(base, QPAD), :]
            minus = table[pl.ds(base + QPAD, QPAD), :]
            both = plus + minus
            if e:
                both = pltpu.roll(both, 64, 1)
            both = both + pltpu.roll(plus - minus, 64 * e + 32, 1)
            total = both if total is None else total + both
        high = total.astype(bf16).astype(f32)
        stacked = jnp.concatenate([high, total - high, high], 0).T.astype(bf16)
        x = jnp.dot(stacked, first_ref[...], preferred_element_type=f32)
        for e in range(2):
            k = 2 * pair + e
            p_re, p_im, m_re, m_im = (
                x[64 * e + 16 * i : 64 * e + 16 * i + 16] for i in range(4)
            )
            t_re = p_re[:, :LANES] - p_im[:, LANES:]
            t_im = m_re[:, LANES:] + m_im[:, :LANES]
            cosine = twist_ref[0, pl.ds(k, 1), :]
            sine = twist_ref[1, pl.ds(k, 1), :]
            v_re = t_re * cosine - t_im * sine
            v_im = t_re * sine + t_im * cosine
            for row, v in ((k, v_re), (KPAD + k, v_im)):
                va[pl.ds(row, cycles, stride=IPITCH), :] = v[:, :128]
                vb[pl.ds(row, cycles, stride=IPITCH), :] = v[:, 128:]
        return carry

    lax.fori_loop(0, KPAD // 2, first_stage, 0, unroll=4)

    rest = FAST - 128

    def last_stage(r, carry):
        base = pl.multiple_of(r * IPITCH, 8)
        rows = pl.ds(base, 2 * KPAD)
        high, low = split(jnp.concatenate([va[rows, :], vb[rows, 0:rest]], 1))
        o = jnp.dot(last_ref[...], high, preferred_element_type=f32)
        o = o[:APAD] + o[APAD:]
        o = o + jnp.dot(last_ref[:APAD], low, preferred_element_type=f32)
        out_ref[r] = o[:SLOW]
        return carry

    lax.fori_loop(0, cycles, last_stage, 0)


def inverse(returned, addr, cycles, scale):
    sources, chunks, rows, wide = returned.shape
    per_chunk = rows // 2
    first, twist, last = inverse_tables(scale)
    vmem = pl.BlockSpec(memory_space=pltpu.VMEM)
    field = pl.pallas_call(
        functools.partial(inverse_kernel, per_chunk, chunks),
        in_specs=[pl.BlockSpec(memory_space=pltpu.SMEM)] + [vmem] * 4,
        out_specs=vmem,
        out_shape=jax.ShapeDtypeStruct((cycles, SLOW, FAST), f32),
        scratch_shapes=[
            pltpu.VMEM((KPAD * 64, 128), f32),
            pltpu.VMEM((128 * BATCH, 128), f32),
            pltpu.VMEM((cycles * IPITCH, 128), f32),
            pltpu.VMEM((cycles * IPITCH, 128), f32),
        ],
        name="inverse",
    )(addr, returned, first, twist, last)
    return field.reshape(cycles, LON)


def exchange(blocks, axis, count, me):
    got = []
    for s in range(1, count):
        block = lax.dynamic_index_in_dim(blocks, lax.rem(me + s, count), 0, keepdims=False)
        got.append(lax.ppermute(block, axis, [(i, (i + s) % count) for i in range(count)]))
    return got


def local(heights, panels, ord_slot, cutoffs):
    lat_count = lax.axis_size("lat")
    ord_count = lax.axis_size("ord")
    me = lax.axis_index("lat")
    cycles = heights.shape[0]
    slots = panels.shape[1]
    order = ord_slot + 1
    rest = order % SLOW
    turn = order // SLOW
    addr = jnp.where(
        rest < HALF, rest * 64 + turn, (SLOW - rest) * 64 + QPAD + turn + 1
    ).astype(jnp.int32)

    picked = forward(heights, addr, ord_count, slots)
    picked = lax.all_to_all(picked, "ord", split_axis=0, concat_axis=0, tiled=True)

    stride = (NMAX - ORDERS) // DEG
    degree_int = ORDERS + np.arange(DEG, dtype=np.int32) * stride
    degree = degree_int.astype(np.float32)
    factors = np.zeros((8, DEG), np.float32)
    factors[0] = 1.0
    factors[1] = (degree + 2.0) / (2.0 * NMAX)
    factors[2] = (degree + 2.0) * (degree + 1.0) / (6.0 * NMAX * NMAX)
    terms = analysis(picked, panels, jnp.asarray(factors), lat_count)

    mine = lax.dynamic_index_in_dim(terms, me, 0, keepdims=False).astype(f32)
    for other in exchange(terms, "lat", lat_count, me):
        mine = mine + other.astype(f32)
    chunks, _, size, _ = mine.shape
    limits = lax.dynamic_index_in_dim(
        cutoffs.reshape(chunks, lat_count, size), me, 1, keepdims=False
    )
    keep = jnp.asarray(degree_int)[None, None, :] <= limits[:, :, None]
    coeffs = jnp.where(keep[:, None], mine, 0.0).astype(bf16)
    pieces = [coeffs]
    for s in range(1, lat_count):
        pairs = [(i, (i + s) % lat_count) for i in range(lat_count)]
        pieces.append(lax.ppermute(coeffs, "lat", pairs))

    back = synthesis(me.astype(jnp.int32).reshape(1), pieces, panels, ord_count, 16 * cycles)
    back = lax.all_to_all(back, "ord", split_axis=0, concat_axis=0, tiled=True)
    cycles_all = cycles * lat_count * ord_count
    return inverse(back, addr, cycles, math.sqrt(cycles_all / (DEG * ORDERS)))


def solution(mesh):
    return jax.shard_map(
        local,
        mesh=mesh,
        in_specs=(P(("lat", "ord"), None), P("lat", "ord", None), P(), P("ord")),
        out_specs=P(("lat", "ord"), None),
        check_vma=False,
    )
```
